512 devices in a mesh: chan: 32 (over z, y_lo), win: 16 (over x, y_hi, core).
Axes of the slice: x: 4, y: 8 (y_hi: 2, y_lo: 4; y = y_hi * 4 + y_lo), z: 8, core: 2. Of those that a mesh axis runs over, the one named last changes fastest.
Arguments:
- spectra: bfloat16 [16, 4096, 1536], P('win', 'chan'), may hold values from -120 to 120
- masks: int32 [16, 4096], replicated, may hold values from 0 to 1, as said below
- matching: int32 [2, 32], replicated, may hold values from 0 to 31, as said below
Outputs:
- corr: bfloat16 [2, 4096, 8192], P(None, ('chan', 'win'))
The draws below stay inside these ranges and needn't reach their ends.
Inputs may be any that keep to these rules, and one draw needn't show every extreme that they name: `masks`: some channels are 0 in every window. `matching`: in round r every block i meets block i XOR s_r, with one s_r for each round, and each bit of 31 is set in exactly one of the two rounds' s_r.
All inputs are finite; a program needn't handle non-finite values.
Results may differ from the reference program's by a relative error of at most 0.014.
Values may be sent and summed in bfloat16 or wider, within the bound.
A program may use at most 64 MiB of HBM per device.

```python
import math
import jax
import jax.numpy as jnp
from jax import lax

CB = 128
F = 768
LAGS = 64
ROUNDS = 2
W_DEV = 1
NBLK = 32
CHANNELS = 4096
WINDOWS = 16
N_WIN = 16


def draw_spectra(key, part):
    first_key, second_key, third_key = jax.random.split(key, 3)
    shape = (WINDOWS, CHANNELS, 2 * F)
    base = jnp.clip(jax.random.normal(first_key, shape, jnp.float32), -5.0, 5.0)
    scale = jnp.exp(jax.random.uniform(second_key, (WINDOWS, CHANNELS, 1), jnp.float32, 0.0, math.log(10.0)))
    rough = jax.random.uniform(third_key, shape, jnp.float32, 0.5, 1.5)
    return (base * scale * rough).astype(jnp.bfloat16)


def draw_masks(key, part):
    first_key, second_key = jax.random.split(jax.random.fold_in(key, 11))
    alive = jax.random.randint(first_key, (1, CHANNELS), 0, 8) != 0
    valid = jax.random.randint(second_key, (WINDOWS, CHANNELS), 0, 8) != 0
    return jnp.logical_and(alive, valid).astype(jnp.int32)


def draw_matching(key, part):
    first = jax.random.randint(jax.random.fold_in(key, 23), (), 1, NBLK - 1).astype(jnp.int32)
    flips = jnp.stack([first, jnp.bitwise_xor(first, NBLK - 1)])
    block_ids = jnp.arange(NBLK, dtype=jnp.int32)
    return jnp.bitwise_xor(block_ids[None, :], flips[:, None]).astype(jnp.int32)


def setup_inputs(seed: int = 0) -> dict:
    splits = jax.random.split(jax.random.key(seed), 4)
    return {
        "spectra": draw_spectra(jax.random.fold_in(splits[3], 71), 0),
        "masks": draw_masks(jax.random.fold_in(splits[3], 71), 0),
        "matching": draw_matching(jax.random.fold_in(splits[3], 71), 0),
    }


def tables(bin_count, lag_count):
    freq = jnp.arange(bin_count, dtype=jnp.int32)
    lag_ids = jnp.arange(lag_count, dtype=jnp.int32)
    phase = lag_ids[:, None] * freq[None, :] % (2 * bin_count)
    angle = phase.astype(jnp.float32) * (math.pi / bin_count)
    return (jnp.cos(angle), jnp.sin(angle))

def rotate(own_rows, cosine, sine):
    bin_count = cosine.shape[1]
    real_part = own_rows[..., :bin_count].astype(jnp.float32)[:, :, None, :]
    imag_part = own_rows[..., bin_count:].astype(jnp.float32)[:, :, None, :]
    turned = jnp.concatenate([real_part * cosine - imag_part * sine, real_part * sine + imag_part * cosine], axis=-1)
    turned = turned.astype(jnp.bfloat16)
    return turned.reshape(own_rows.shape[0], own_rows.shape[1] * cosine.shape[0], 2 * bin_count)

def whiten(spectra, flags):
    values = spectra.astype(jnp.float32)
    mean_square = lax.optimization_barrier(jnp.mean(values * values, axis=-1, keepdims=True))
    return (flags.astype(jnp.float32)[..., None] * values * lax.rsqrt(mean_square + 1e-06)).astype(jnp.bfloat16)

def reference(spectra, masks, matching):
    whitened = whiten(spectra, masks)
    cosine, sine = tables(F, LAGS)
    flags = masks.astype(jnp.bfloat16)

    def one_block(index):
        round_id = index // NBLK
        block_id = index % NBLK
        partner = matching[round_id, block_id]
        own_spec = lax.dynamic_slice_in_dim(whitened, (block_id * CB).astype(jnp.int32), CB, 1)
        other_spec = lax.dynamic_slice_in_dim(whitened, (partner * CB).astype(jnp.int32), CB, 1)
        own_cols = lax.dynamic_slice_in_dim(flags, (block_id * CB).astype(jnp.int32), CB, 1)
        other_cols = lax.dynamic_slice_in_dim(flags, (partner * CB).astype(jnp.int32), CB, 1)
        counts = lax.dot_general(own_cols, other_cols, (((0,), (0,)), ((), ())), preferred_element_type=jnp.float32)

        def group(running, group_id):
            first = (group_id * W_DEV).astype(jnp.int32)
            own_group = lax.dynamic_slice_in_dim(own_spec, first, W_DEV, 0)
            other_group = lax.dynamic_slice_in_dim(other_spec, first, W_DEV, 0)
            rotated = rotate(own_group, cosine, sine)
            term = jnp.einsum('wxk,wbk->xb', rotated.astype(jnp.float32), other_group.astype(jnp.float32))
            return (running + lax.optimization_barrier(term.astype(jnp.bfloat16)).astype(jnp.float32), None)
        running, _ = lax.scan(group, jnp.zeros((CB * LAGS, CB), jnp.float32), jnp.arange(N_WIN, dtype=jnp.int32))
        stacked = running.reshape(CB, LAGS, CB)
        scale = jnp.sqrt(F * jnp.maximum(counts, 1.0))
        return (stacked / scale[:, None, :]).reshape(CB, LAGS * CB).astype(jnp.bfloat16)
    result = lax.map(one_block, jnp.arange(ROUNDS * NBLK, dtype=jnp.int32))
    return result.reshape(ROUNDS, CHANNELS, LAGS * CB)
```

```python
import functools
import math

import jax
import jax.numpy as jnp
import numpy as np
from jax import lax
from jax.experimental import pallas as pl
from jax.experimental.pallas import tpu as pltpu
from jax.sharding import PartitionSpec as P

LAGS = 64
ROUNDS = 2
FINE = 16
COARSE = LAGS // FINE
MESH = pl.DeviceIdType.MESH

FAR_UP, FAR_DOWN, OWN_UP, OWN_DOWN, SUM_UP, SUM_DOWN, ACROSS = range(7)


def tables(bin_count):
    freq = np.arange(bin_count, dtype=np.int64)
    fine = np.arange(FINE, dtype=np.int64)[:, None]
    coarse = FINE * np.arange(COARSE, dtype=np.int64)[:, None]
    lags = np.concatenate([fine, coarse], axis=0)
    angle = (lags * freq % (2 * bin_count)).astype(np.float64) * (math.pi / bin_count)
    return np.cos(angle).astype(np.float32), np.sin(angle).astype(np.float32)


def stack_kernel(own_ref, part_ref, cos_ref, sin_ref, scale_ref, out_ref, own_rx, part_rx, lhs, rhs,
                 mine, held, sends, gets, pair_send, pair_recv, ssem, rsem):
    chan = lax.axis_index("chan")
    win = lax.axis_index("win")
    x_pos = win // 4
    y_pos = (win // 2) % 2
    core = win % 2
    up = (chan, (win + 4) % 16)
    down = (chan, (win + 12) % 16)
    across = (chan, win + 2 - 4 * y_pos)
    twin = (chan, win + 1 - 2 * core)
    bins = own_ref.shape[1] // 2
    rows = FINE * 8

    barrier = pltpu.get_barrier_semaphore()
    for device in (up, down, across, twin):
        pl.semaphore_signal(barrier, inc=1, device_id=device, device_id_type=MESH)
    pl.semaphore_wait(barrier, 4)

    pair_copies = [
        pltpu.make_async_remote_copy(src, dst, pair_send.at[k], pair_recv.at[k], device_id=twin,
                                     device_id_type=MESH)
        for k, (src, dst) in enumerate(
            [(own_ref, own_rx), (part_ref.at[0], part_rx.at[0]), (part_ref.at[1], part_rx.at[1])])
    ]
    for copy in pair_copies:
        copy.start()

    def rotate_own(src, slot):
        @pl.loop(0, 8)
        def _(group):
            both = src[pl.ds(pl.multiple_of(group * 16, 16), 16), :].astype(jnp.float32)
            own = jnp.where(core == 0, both[:8], both[8:])
            real, imag = own[:, :bins], own[:, bins:]
            for pair in range(FINE // 2):
                reals, imags = [], []
                for lag in (2 * pair, 2 * pair + 1):
                    cosine, sine = cos_ref[lag : lag + 1, :], sin_ref[lag : lag + 1, :]
                    reals.append(real * cosine - imag * sine)
                    imags.append(real * sine + imag * cosine)
                at = pl.ds(pl.multiple_of(group * rows + pair * 16, 16), 16)
                lhs[at, slot * 2 * bins : slot * 2 * bins + bins] = jnp.concatenate(
                    reals, axis=0).astype(jnp.bfloat16)
                lhs[at, slot * 2 * bins + bins : (slot + 1) * 2 * bins] = jnp.concatenate(
                    imags, axis=0).astype(jnp.bfloat16)

    def rotate_other(src, round_id, slot):
        @pl.loop(0, 8)
        def _(group):
            block = src[pl.ds(pl.multiple_of(group * 16, 16), 16), :].astype(jnp.float32)
            real, imag = block[:, :bins], block[:, bins:]
            for lag in range(COARSE):
                cosine = cos_ref[FINE + lag : FINE + lag + 1, :]
                sine = sin_ref[FINE + lag : FINE + lag + 1, :]
                at = pl.ds(
                    pl.multiple_of((round_id * COARSE + lag) * 128 + group * 16, 16), 16)
                rhs[at, slot * 2 * bins : slot * 2 * bins + bins] = (
                    real * cosine + imag * sine).astype(jnp.bfloat16)
                rhs[at, slot * 2 * bins + bins : (slot + 1) * 2 * bins] = (
                    imag * cosine - real * sine).astype(jnp.bfloat16)

    rotate_own(own_ref, 0)
    rotate_other(part_ref.at[0], 0, 0)
    rotate_other(part_ref.at[1], 1, 0)
    pair_copies[0].wait_recv()
    rotate_own(own_rx, 1)
    pair_copies[1].wait_recv()
    rotate_other(part_rx.at[0], 0, 1)
    pair_copies[2].wait_recv()
    rotate_other(part_rx.at[1], 1, 1)

    def copy_of(kind, piece):
        device = (up, down, up, down, up, down, across)[kind]
        return pltpu.make_async_remote_copy(
            sends.at[piece, kind], gets.at[piece, kind], ssem.at[piece, kind],
            rsem.at[piece, kind], device_id=device, device_id_type=MESH)

    def product(piece, x_to):
        left = lhs[pl.ds(pl.multiple_of(x_to * 2 * rows, 2 * rows), 2 * rows), :]
        right = rhs[pl.ds(pl.multiple_of(piece * 256, 256), 256), :]
        return lax.dot_general(left, right, (((1,), (1,)), ((), ())),
                               preferred_element_type=jnp.float32)

    def compute(piece):
        far = product(piece, (x_pos + 2) % 4)
        sends[piece, FAR_UP] = far[:rows].astype(jnp.bfloat16)
        sends[piece, FAR_DOWN] = far[rows:].astype(jnp.bfloat16)
        copy_of(FAR_UP, piece).start()
        copy_of(FAR_DOWN, piece).start()
        near = product(piece, (x_pos + 1) % 4)
        held[piece, 0] = near[:rows]
        sends[piece, OWN_UP] = near[rows:].astype(jnp.bfloat16)
        copy_of(OWN_UP, piece).start()
        near = product(piece, (x_pos + 3) % 4)
        sends[piece, OWN_DOWN] = near[:rows].astype(jnp.bfloat16)
        copy_of(OWN_DOWN, piece).start()
        held[piece, 1] = near[rows:]
        own = product(piece, x_pos)
        mine[piece, 0] = own[:rows]
        mine[piece, 1] = own[rows:]

    def pass_on(piece):
        for kind, far in ((SUM_UP, FAR_UP), (SUM_DOWN, FAR_DOWN)):
            copy_of(far, piece).wait_recv()
            total = held[piece, kind - SUM_UP] + gets[piece, far].astype(jnp.float32)
            sends[piece, kind] = total.astype(jnp.bfloat16)
            copy_of(kind, piece).start()

    def along_x(piece, y_to):
        return (mine[piece, y_to] + gets[piece, SUM_UP + y_to].astype(jnp.float32)
                + gets[piece, OWN_DOWN - y_to].astype(jnp.float32))

    def cross(piece):
        for kind in (OWN_UP, OWN_DOWN, SUM_UP, SUM_DOWN):
            copy_of(kind, piece).wait_recv()
        sends[piece, ACROSS] = along_x(piece, 1 - y_pos).astype(jnp.bfloat16)
        copy_of(ACROSS, piece).start()
        mine[piece, y_pos] = along_x(piece, y_pos)

    def finish(piece):
        copy_of(ACROSS, piece).wait_recv()
        total = mine[piece, y_pos] + gets[piece, ACROSS].astype(jnp.float32)
        round_id = piece // 2
        scale = scale_ref[round_id]
        for half in range(2):
            for fine in range(FINE):
                block = total[fine * 8 : fine * 8 + 8, half * 128 : half * 128 + 128] * scale
                lag = ((piece % 2) * 2 + half) * FINE + fine
                at = pl.ds(pl.multiple_of(lag * 128, 128), 128)
                out_ref[round_id, :, at] = block.astype(jnp.bfloat16)

    pieces = ROUNDS * 2

    @pl.loop(0, pieces + 3)
    def _(step):
        @pl.when(step < pieces)
        def _():
            compute(step)

        @pl.when(jnp.logical_and(step >= 1, step < pieces + 1))
        def _():
            pass_on(step - 1)

        @pl.when(jnp.logical_and(step >= 2, step < pieces + 2))
        def _():
            cross(step - 2)

        @pl.when(step >= 3)
        def _():
            finish(step - 3)

    for copy in pair_copies:
        copy.wait_send()

    @pl.loop(0, pieces)
    def _(piece):
        for kind in range(7):
            copy_of(kind, piece).wait_send()


def stack(own, partners, scale):
    block_rows, two_bins = own.shape
    bins = two_bins // 2
    cosine, sine = tables(bins)
    rows = FINE * 8
    pieces = 4
    bf16, f32 = jnp.bfloat16, jnp.float32
    return pl.pallas_call(
        stack_kernel,
        name="stack",
        out_shape=jax.ShapeDtypeStruct((ROUNDS, 8, LAGS * block_rows), bf16),
        in_specs=[pl.BlockSpec(memory_space=pltpu.VMEM)] * 5,
        out_specs=pl.BlockSpec(memory_space=pltpu.VMEM),
        scratch_shapes=[
            pltpu.VMEM((block_rows, two_bins), bf16),
            pltpu.VMEM((ROUNDS, block_rows, two_bins), bf16),
            pltpu.VMEM((8 * rows, 2 * two_bins), bf16),
            pltpu.VMEM((ROUNDS * COARSE * block_rows, 2 * two_bins), bf16),
            pltpu.VMEM((pieces, 2, rows, 256), f32),
            pltpu.VMEM((pieces, 2, rows, 256), f32),
            pltpu.VMEM((pieces, 7, rows, 256), bf16),
            pltpu.VMEM((pieces, 7, rows, 256), bf16),
            pltpu.SemaphoreType.DMA((3,)),
            pltpu.SemaphoreType.DMA((3,)),
            pltpu.SemaphoreType.DMA((pieces, 7)),
            pltpu.SemaphoreType.DMA((pieces, 7)),
        ],
        compiler_params=pltpu.CompilerParams(
            collective_id=0, has_side_effects=True, vmem_limit_bytes=48 << 20),
    )(own, partners, jnp.asarray(cosine), jnp.asarray(sine), scale)


def partner_2(value, axis, apart):
    mask = 2**apart
    pairs = [(source, source ^ mask) for source in range(lax.axis_size(axis))]
    return lax.ppermute(value, axis, pairs)


def whiten(spectra, flags):
    values = spectra.astype(jnp.float32)
    mean_square = jnp.mean(values * values, axis=-1, keepdims=True)
    return (flags.astype(jnp.float32)[..., None] * values * lax.rsqrt(mean_square + 1e-06)).astype(
        jnp.bfloat16
    )


def deliver(values, flip_bits):
    levels = lax.axis_size("chan").bit_length() - 1
    first, second = values, values
    for bit_number in range(levels):
        taken = jnp.right_shift(flip_bits, bit_number) & 1 == 1
        moved = partner_2(jnp.where(taken, first, second), "chan", bit_number)
        first = jnp.where(taken, moved, first)
        second = jnp.where(taken, second, moved)
    return first, second


def shards(spectra, masks, matching):
    block_id = lax.axis_index("chan")
    slot_id = lax.axis_index("win")
    win_count = lax.axis_size("win")
    w_count, block_rows, two_bins = spectra.shape
    bin_count = two_bins // 2
    row_count = block_rows // win_count
    own_flags = lax.dynamic_slice(
        masks, (slot_id * w_count, block_id * block_rows), (w_count, block_rows)
    )
    whitened = whiten(spectra, own_flags)[0]
    flags = masks.astype(jnp.bfloat16)
    own_cols = lax.dynamic_slice_in_dim(
        flags, block_id * block_rows + slot_id * row_count, row_count, 1)
    scales = []
    for round_id in range(ROUNDS):
        partner = matching[round_id, block_id]
        other_cols = lax.dynamic_slice_in_dim(flags, partner * block_rows, block_rows, 1)
        counts = lax.dot_general(
            own_cols, other_cols, (((0,), (0,)), ((), ())), preferred_element_type=jnp.float32
        )
        scales.append(lax.rsqrt(bin_count * jnp.maximum(counts, 1.0)))
    first, second = deliver(whitened, jnp.bitwise_xor(matching[0, block_id], block_id))
    return stack(whitened, jnp.stack([first, second]), jnp.stack(scales))


def solution(mesh):
    in_specs = (P("win", "chan", None), P(), P())
    out_specs = P(None, ("chan", "win"), None)
    return jax.shard_map(shards, mesh=mesh, in_specs=in_specs, out_specs=out_specs, check_vma=False)
```

```python
import functools
import math

import jax
import jax.numpy as jnp
import numpy as np
from jax import lax
from jax.experimental import pallas as pl
from jax.experimental.pallas import tpu as pltpu
from jax.sharding import PartitionSpec as P

LAGS = 64
ROUNDS = 2
FINE = 16
COARSE = LAGS // FINE
MESH = pl.DeviceIdType.MESH

CHUNKS = 4
PIECES = ROUNDS * 2

FAR_UP, FAR_DOWN, OWN_UP, OWN_DOWN, SUM_UP, SUM_DOWN, ACROSS = range(7)


def tables(bin_count):
    freq = np.arange(bin_count, dtype=np.int64)
    fine = np.arange(FINE, dtype=np.int64)[:, None]
    coarse = FINE * np.arange(COARSE, dtype=np.int64)[:, None]
    lags = np.concatenate([fine, coarse], axis=0)
    angle = (lags * freq % (2 * bin_count)).astype(np.float64) * (math.pi / bin_count)
    return np.cos(angle).astype(np.float32), np.sin(angle).astype(np.float32)


def stack_kernel(flips, spec_ref, masks_ref, cos_ref, sin_ref, out_ref, flag, counts, own, parts,
                 lhs, rhs, prod, cast, sums, gets, own_sem, part_send, part_recv, twin_send,
                 twin_recv, ssem, rsem):
    chan = lax.axis_index("chan")
    win = lax.axis_index("win")
    x_pos = win // 4
    y_pos = (win // 2) % 2
    core = win % 2
    up = (chan, (win + 4) % 16)
    down = (chan, (win + 12) % 16)
    across = (chan, win + 2 - 4 * y_pos)
    twin = (chan, win + 1 - 2 * core)
    partners = [jnp.bitwise_xor(chan, flip) for flip in flips]
    bins = spec_ref.shape[2] // 2
    block_rows = spec_ref.shape[1]
    chunk_rows = block_rows // CHUNKS
    rows = FINE * 8

    barrier = pltpu.get_barrier_semaphore()
    greeted = [up, down, across, twin]
    greeted += [(partner, win) for partner, flip in zip(partners, flips) if flip]
    for device in greeted:
        pl.semaphore_signal(barrier, inc=1, device_id=device, device_id_type=MESH)

    def columns(block_id):
        return pl.ds(pl.multiple_of(block_id * block_rows, block_rows), block_rows)

    own_flags = masks_ref[:, columns(chan)].astype(jnp.float32)
    windows = lax.broadcasted_iota(jnp.int32, own_flags.shape, 0)
    row = jnp.sum(jnp.where(windows == win, own_flags, 0.0), axis=0, keepdims=True)
    own_flags = own_flags.astype(jnp.bfloat16)
    shape = (block_rows, block_rows)
    diagonal = lax.broadcasted_iota(jnp.int32, shape, 0) == lax.broadcasted_iota(
        jnp.int32, shape, 1)
    flag[...] = jnp.sum(
        jnp.where(diagonal, jnp.broadcast_to(row, shape), 0.0), axis=1, keepdims=True)

    @pl.loop(0, block_rows // 16)
    def _(group):
        at = pl.ds(pl.multiple_of(group * 16, 16), 16)
        values = spec_ref[0, at, :].astype(jnp.float32)
        mean_square = jnp.mean(values * values, axis=-1, keepdims=True)
        own[0, at, :] = (flag[at, :] * values * lax.rsqrt(mean_square + 1e-06)).astype(
            jnp.bfloat16)

    pl.semaphore_wait(barrier, len(greeted))

    def chunk(index):
        return pl.ds(pl.multiple_of(index * chunk_rows, chunk_rows), chunk_rows)

    def part_copy(role, index, partner):
        return pltpu.make_async_remote_copy(
            own.at[0, chunk(index)], parts.at[0, role, chunk(index)], part_send.at[role, index],
            part_recv.at[role, index], device_id=(partner, win), device_id_type=MESH)

    def twin_copy(role, index):
        return pltpu.make_async_remote_copy(
            parts.at[0, role, chunk(index)], parts.at[1, role, chunk(index)],
            twin_send.at[role, index], twin_recv.at[role, index], device_id=twin,
            device_id_type=MESH)

    for role, (partner, flip) in enumerate(zip(partners, flips)):
        @pl.loop(0, CHUNKS)
        def _(index):
            if flip:
                part_copy(role, index, partner).start()
            else:
                pltpu.make_async_copy(own.at[0, chunk(index)], parts.at[0, role, chunk(index)],
                                      part_recv.at[role, index]).start()
    own_copy = pltpu.make_async_remote_copy(own.at[0], own.at[1], own_sem.at[0], own_sem.at[1],
                                            device_id=twin, device_id_type=MESH)
    own_copy.start()

    for role, partner in enumerate(partners):
        other = masks_ref[:, columns(partner)].astype(jnp.float32).astype(jnp.bfloat16)
        both = lax.dot_general(own_flags, other, (((0,), (0,)), ((), ())),
                               preferred_element_type=jnp.float32)
        counts[role] = lax.rsqrt(bins * jnp.maximum(both, 1.0))

    @pl.loop(0, 2)
    def _(slot):
        @pl.when(slot == 1)
        def _():
            own_copy.wait_recv()

        left = pl.ds(pl.multiple_of(slot * 2 * bins, 128), bins)
        right = pl.ds(pl.multiple_of(slot * 2 * bins + bins, 128), bins)

        @pl.loop(0, 8)
        def _(group):
            both = own[slot, pl.ds(pl.multiple_of(group * 16, 16), 16), :].astype(jnp.float32)
            mine = jnp.where(core == 0, both[:8], both[8:])
            real, imag = mine[:, :bins], mine[:, bins:]
            for pair in range(FINE // 2):
                reals, imags = [], []
                for lag in (2 * pair, 2 * pair + 1):
                    cosine, sine = cos_ref[lag : lag + 1, :], sin_ref[lag : lag + 1, :]
                    reals.append(real * cosine - imag * sine)
                    imags.append(real * sine + imag * cosine)
                at = pl.ds(pl.multiple_of(group * rows + pair * 16, 16), 16)
                lhs[at, left] = jnp.concatenate(reals, axis=0).astype(jnp.bfloat16)
                lhs[at, right] = jnp.concatenate(imags, axis=0).astype(jnp.bfloat16)

    def copy_of(kind, piece):
        source = (cast.at[piece, 0, 0], cast.at[piece, 0, 1], cast.at[piece, 1, 1],
                  cast.at[piece, 3, 0], sums.at[piece, 0], sums.at[piece, 1],
                  sums.at[piece, 2])[kind]
        device = (up, down, up, down, up, down, across)[kind]
        return pltpu.make_async_remote_copy(
            source, gets.at[piece, kind], ssem.at[piece, kind], rsem.at[piece, kind],
            device_id=device, device_id_type=MESH)

    def compute(piece):
        @pl.loop(0, 4)
        def _(step):
            x_to = (x_pos + 6 - step) % 4
            left = lhs[pl.ds(pl.multiple_of(x_to * 2 * rows, 2 * rows), 2 * rows), :]
            right = rhs[pl.ds(pl.multiple_of(piece * 256, 256), 256), :]
            product = lax.dot_general(left, right, (((1,), (1,)), ((), ())),
                                      preferred_element_type=jnp.float32)
            for half in range(2):
                value = product[half * rows : (half + 1) * rows]
                prod[piece, step, half] = value
                cast[piece, step, half] = value.astype(jnp.bfloat16)

            @pl.when(step == 0)
            def _():
                copy_of(FAR_UP, piece).start()
                copy_of(FAR_DOWN, piece).start()

            @pl.when(step == 1)
            def _():
                copy_of(OWN_UP, piece).start()

            @pl.when(step == 3)
            def _():
                copy_of(OWN_DOWN, piece).start()

    def pass_on(piece):
        for side, (kind, far) in enumerate(((SUM_UP, FAR_UP), (SUM_DOWN, FAR_DOWN))):
            copy_of(far, piece).wait_recv()
            total = prod[piece, 1 + 2 * side, side] + gets[piece, far].astype(jnp.float32)
            sums[piece, side] = total.astype(jnp.bfloat16)
            copy_of(kind, piece).start()

    def along_x(piece, y_to):
        return (prod[piece, 2, y_to] + gets[piece, SUM_UP + y_to].astype(jnp.float32)
                + gets[piece, OWN_DOWN - y_to].astype(jnp.float32))

    def cross(piece):
        for kind in (OWN_UP, OWN_DOWN, SUM_UP, SUM_DOWN):
            copy_of(kind, piece).wait_recv()
        sums[piece, 2] = along_x(piece, 1 - y_pos).astype(jnp.bfloat16)
        copy_of(ACROSS, piece).start()
        prod[piece, 2, y_pos] = along_x(piece, y_pos)

    def finish(piece):
        copy_of(ACROSS, piece).wait_recv()
        total = prod[piece, 2, y_pos] + gets[piece, ACROSS].astype(jnp.float32)
        role = piece // 2
        scale = counts[role, pl.ds(pl.multiple_of(win * 8, 8), 8), :]
        for half in range(2):
            for fine in range(FINE):
                block = total[fine * 8 : fine * 8 + 8, half * 128 : half * 128 + 128] * scale
                lag = ((piece % 2) * 2 + half) * FINE + fine
                at = pl.ds(pl.multiple_of(lag * 128, 128), 128)
                out_ref[role, :, at] = block.astype(jnp.bfloat16)

    @pl.loop(0, ROUNDS)
    def _(role):
        @pl.loop(0, 2 * CHUNKS)
        def _(step):
            slot, index = step // CHUNKS, step % CHUNKS

            @pl.when(slot == 0)
            def _():
                part_copy(role, index, partners[1]).wait_recv()
                twin_copy(role, index).start()

            @pl.when(slot == 1)
            def _():
                twin_copy(role, index).wait_recv()

            left = pl.ds(pl.multiple_of(slot * 2 * bins, 128), bins)
            right = pl.ds(pl.multiple_of(slot * 2 * bins + bins, 128), bins)

            @pl.loop(0, chunk_rows // 16)
            def _(group):
                first = index * chunk_rows + group * 16
                block = parts[slot, role, pl.ds(pl.multiple_of(first, 16), 16), :].astype(
                    jnp.float32)
                real, imag = block[:, :bins], block[:, bins:]
                for lag in range(COARSE):
                    cosine = cos_ref[FINE + lag : FINE + lag + 1, :]
                    sine = sin_ref[FINE + lag : FINE + lag + 1, :]
                    at = pl.ds(
                        pl.multiple_of((role * COARSE + lag) * block_rows + first, 16), 16)
                    rhs[at, left] = (real * cosine + imag * sine).astype(jnp.bfloat16)
                    rhs[at, right] = (imag * cosine - real * sine).astype(jnp.bfloat16)

        @pl.when(role == 1)
        def _():
            cross(0)
            cross(1)

        @pl.loop(0, 2)
        def _(half):
            compute(2 * role + half)

        @pl.loop(0, 2)
        def _(half):
            pass_on(2 * role + half)

    @pl.loop(0, PIECES)
    def _(piece):
        @pl.when(piece < 2)
        def _():
            cross(piece + 2)

        finish(piece)

    own_copy.wait_send()

    @pl.loop(0, CHUNKS)
    def _(index):
        for role, (partner, flip) in enumerate(zip(partners, flips)):
            if flip:
                part_copy(role, index, partner).wait_send()
            twin_copy(role, index).wait_send()

    @pl.loop(0, PIECES)
    def _(piece):
        for kind in range(7):
            copy_of(kind, piece).wait_send()


def correlate(flip, spectra, masks, cosine, sine):
    block_rows, two_bins = spectra.shape[1:]
    rows = FINE * 8
    bf16, f32 = jnp.bfloat16, jnp.float32
    vmem, dma = pltpu.VMEM, pltpu.SemaphoreType.DMA
    return pl.pallas_call(
        functools.partial(stack_kernel, (flip, flip ^ (lax.axis_size("chan") - 1))),
        name=f"stack_{flip}",
        out_shape=jax.ShapeDtypeStruct((ROUNDS, 8, LAGS * block_rows), bf16),
        in_specs=[pl.BlockSpec(memory_space=vmem)] * 4,
        out_specs=pl.BlockSpec(memory_space=vmem),
        scratch_shapes=[
            vmem((block_rows, 1), f32),
            vmem((ROUNDS, block_rows, block_rows), f32),
            vmem((2, block_rows, two_bins), bf16),
            vmem((2, ROUNDS, block_rows, two_bins), bf16),
            vmem((8 * rows, 2 * two_bins), bf16),
            vmem((ROUNDS * COARSE * block_rows, 2 * two_bins), bf16),
            vmem((PIECES, 4, 2, rows, 256), f32),
            vmem((PIECES, 4, 2, rows, 256), bf16),
            vmem((PIECES, 3, rows, 256), bf16),
            vmem((PIECES, 7, rows, 256), bf16),
            dma((2,)),
            dma((ROUNDS, CHUNKS)),
            dma((ROUNDS, CHUNKS)),
            dma((ROUNDS, CHUNKS)),
            dma((ROUNDS, CHUNKS)),
            dma((PIECES, 7)),
            dma((PIECES, 7)),
        ],
        compiler_params=pltpu.CompilerParams(
            collective_id=flip, has_side_effects=True, vmem_limit_bytes=48 << 20),
    )(spectra, masks, cosine, sine)


def shards(spectra, masks, matching):
    blocks = lax.axis_size("chan")
    cosine, sine = tables(spectra.shape[2] // 2)
    distance = matching[0, 0]
    turned = distance >= blocks // 2
    lower = jnp.where(turned, blocks - 1 - distance, distance)
    branches = [functools.partial(correlate, flip) for flip in range(blocks // 2)]
    result = lax.switch(lower, branches, spectra, masks, jnp.asarray(cosine), jnp.asarray(sine))
    return jnp.where(turned, jnp.flip(result, axis=0), result)


def solution(mesh):
    in_specs = (P("win", "chan", None), P(), P())
    out_specs = P(None, ("chan", "win"), None)
    return jax.shard_map(shards, mesh=mesh, in_specs=in_specs, out_specs=out_specs, check_vma=False)
```

```python
import functools
import math

import jax
import jax.numpy as jnp
import numpy as np
from jax import lax
from jax.experimental import pallas as pl
from jax.experimental.pallas import tpu as pltpu
from jax.sharding import PartitionSpec as P

LAGS = 64
ROUNDS = 2
FINE = 16
COARSE = LAGS // FINE
MESH = pl.DeviceIdType.MESH

PIECES = 4

FAR_UP, FAR_DOWN, OWN_UP, OWN_DOWN, SUM_UP, SUM_DOWN, ACROSS = range(7)


def tables(bin_count):
    freq = np.arange(bin_count, dtype=np.int64)
    fine = np.arange(FINE, dtype=np.int64)[:, None]
    coarse = FINE * np.arange(COARSE, dtype=np.int64)[:, None]
    lags = np.concatenate([fine, coarse], axis=0)
    angle = (lags * freq % (2 * bin_count)).astype(np.float64) * (math.pi / bin_count)
    return np.cos(angle).astype(np.float32), np.sin(angle).astype(np.float32)


def stack_kernel(route, spec_ref, masks_ref, cos_ref, sin_ref, out_ref, flag, counts,
                 own, parts, hop, lhs, rhs, prod, cast, sums, gets, own_sem, hop_send, hop_recv, part_send,
                 part_recv, twin_send, twin_recv, ssem, rsem):
    flips, first_hop, steps = route
    chan = lax.axis_index("chan")
    win = lax.axis_index("win")
    x_pos = win // 4
    y_pos = (win // 2) % 2
    core = win % 2
    up = (chan, (win + 4) % 16)
    down = (chan, (win + 12) % 16)
    across = (chan, win + 2 - 4 * y_pos)
    twin = (chan, win + 1 - 2 * core)
    bins = spec_ref.shape[2] // 2
    block_rows = spec_ref.shape[1]
    chunk_rows = block_rows // PIECES
    rows = FINE * 8

    barrier = pltpu.get_barrier_semaphore()
    greeted = [up, down, across, twin]
    greeted += [(jnp.bitwise_xor(chan, flip), win) for flip in (first_hop, *steps) if flip]
    for device in greeted:
        pl.semaphore_signal(barrier, inc=1, device_id=device, device_id_type=MESH)

    def columns(block_id):
        return pl.ds(pl.multiple_of(block_id * block_rows, block_rows), block_rows)

    own_flags = masks_ref[:, columns(chan)].astype(jnp.float32)
    windows = lax.broadcasted_iota(jnp.int32, own_flags.shape, 0)
    row = jnp.sum(jnp.where(windows == win, own_flags, 0.0), axis=0, keepdims=True)
    own_flags = own_flags.astype(jnp.bfloat16)
    shape = (block_rows, block_rows)
    diagonal = lax.broadcasted_iota(jnp.int32, shape, 0) == lax.broadcasted_iota(
        jnp.int32, shape, 1)
    flag[...] = jnp.sum(
        jnp.where(diagonal, jnp.broadcast_to(row, shape), 0.0), axis=1, keepdims=True)

    @pl.loop(0, block_rows // 16)
    def _(group):
        at = pl.ds(pl.multiple_of(group * 16, 16), 16)
        values = spec_ref[0, at, :].astype(jnp.float32)
        mean_square = jnp.mean(values * values, axis=-1, keepdims=True)
        own[0, at, :] = (flag[at, :] * values * lax.rsqrt(mean_square + 1e-06)).astype(
            jnp.bfloat16)

    pl.semaphore_wait(barrier, len(greeted))

    def chunk(index):
        return pl.ds(pl.multiple_of(index * chunk_rows, chunk_rows), chunk_rows)

    landing = hop if first_hop and steps[0] else parts.at[0, 0]
    source = landing if first_hop else own.at[0]

    def hop_copy(index):
        return pltpu.make_async_remote_copy(
            own.at[0, chunk(index)], landing.at[chunk(index)], hop_send.at[index],
            hop_recv.at[index], device_id=(jnp.bitwise_xor(chan, first_hop), win),
            device_id_type=MESH)

    def part_copy(role, index, flip):
        return pltpu.make_async_remote_copy(
            source.at[chunk(index)], parts.at[0, role, chunk(index)], part_send.at[role, index],
            part_recv.at[role, index], device_id=(jnp.bitwise_xor(chan, flip), win),
            device_id_type=MESH)

    def hop_on(index):
        hop_copy(index).wait_recv()
        for role, flip in enumerate(steps):
            if flip:
                part_copy(role, index, flip).start()

    def twin_copy(role, index):
        return pltpu.make_async_remote_copy(
            parts.at[0, role, chunk(index)], parts.at[1, role, chunk(index)],
            twin_send.at[role, index], twin_recv.at[role, index], device_id=twin,
            device_id_type=MESH)

    if first_hop:
        @pl.loop(0, PIECES)
        def _(index):
            hop_copy(index).start()
    else:
        @pl.loop(0, PIECES)
        def _(index):
            for role, flip in enumerate(steps):
                if flip:
                    part_copy(role, index, flip).start()
                else:
                    pltpu.make_async_copy(own.at[0, chunk(index)],
                                          parts.at[0, role, chunk(index)],
                                          part_recv.at[role, index]).start()
    own_copy = pltpu.make_async_remote_copy(own.at[0], own.at[1], own_sem.at[0], own_sem.at[1],
                                            device_id=twin, device_id_type=MESH)
    own_copy.start()

    def halves(slot):
        return (pl.ds(pl.multiple_of(slot * 2 * bins, 128), bins),
                pl.ds(pl.multiple_of(slot * 2 * bins + bins, 128), bins))

    def rotate_own(slot, group):
        left, right = halves(slot)
        both = own[slot, pl.ds(pl.multiple_of(group * 16, 16), 16), :].astype(jnp.float32)
        mine = jnp.where(core == 0, both[:8], both[8:])
        real, imag = mine[:, :bins], mine[:, bins:]
        place = ((group // 2 - x_pos + 3) % 4) * 2 + group % 2
        for pair in range(FINE // 2):
            reals, imags = [], []
            for lag in (2 * pair, 2 * pair + 1):
                cosine, sine = cos_ref[lag : lag + 1, :], sin_ref[lag : lag + 1, :]
                reals.append(real * cosine - imag * sine)
                imags.append(real * sine + imag * cosine)
            at = pl.ds(pl.multiple_of(place * rows + pair * 16, 16), 16)
            lhs[at, left] = jnp.concatenate(reals, axis=0).astype(jnp.bfloat16)
            lhs[at, right] = jnp.concatenate(imags, axis=0).astype(jnp.bfloat16)

    @pl.loop(0, PIECES * 4)
    def _(step):
        @pl.when(step == PIECES * 2)
        def _():
            own_copy.wait_recv()

        if first_hop:
            @pl.when(jnp.logical_and(step >= PIECES * 2, step % 4 == 0))
            def _():
                hop_on(step // 4 - PIECES // 2)

        rotate_own(step // (PIECES * 2), step % (PIECES * 2))

    for role, flip in enumerate(flips):
        other = masks_ref[:, columns(jnp.bitwise_xor(chan, flip))]
        other = other.astype(jnp.float32).astype(jnp.bfloat16)
        both = lax.dot_general(own_flags, other, (((0,), (0,)), ((), ())),
                               preferred_element_type=jnp.float32)
        counts[role] = lax.rsqrt(bins * jnp.maximum(both, 1.0))

    def rotate_other(slot, piece):
        left, right = halves(slot)
        groups = chunk_rows // 16

        @pl.loop(0, ROUNDS * groups)
        def _(step):
            role, first = step // groups, (step % groups) * 16
            at = pl.ds(pl.multiple_of(piece * chunk_rows + first, 16), 16)
            block = parts[slot, role, at, :].astype(jnp.float32)
            real, imag = block[:, :bins], block[:, bins:]
            for lag in range(COARSE):
                cosine = cos_ref[FINE + lag : FINE + lag + 1, :]
                sine = sin_ref[FINE + lag : FINE + lag + 1, :]
                at = piece * 256 + role * block_rows + lag * chunk_rows + first
                at = pl.ds(pl.multiple_of(at, 16), 16)
                rhs[at, left] = (real * cosine + imag * sine).astype(jnp.bfloat16)
                rhs[at, right] = (imag * cosine - real * sine).astype(jnp.bfloat16)

    def copy_of(kind, piece):
        source = (cast.at[piece, 1, 0], cast.at[piece, 1, 1], cast.at[piece, 0, 1],
                  cast.at[piece, 2, 0], sums.at[piece, 0], sums.at[piece, 1],
                  sums.at[piece, 2])[kind]
        device = (up, down, up, down, up, down, across)[kind]
        return pltpu.make_async_remote_copy(
            source, gets.at[piece, kind], ssem.at[piece, kind], rsem.at[piece, kind],
            device_id=device, device_id_type=MESH)

    def compute(piece):
        @pl.loop(0, 2)
        def _(step):
            left = lhs[pl.ds(pl.multiple_of(step * 4 * rows, 4 * rows), 4 * rows), :]
            right = rhs[pl.ds(pl.multiple_of(piece * 256, 256), 256), :]
            product = lax.dot_general(left, right, (((1,), (1,)), ((), ())),
                                      preferred_element_type=jnp.float32)
            for part in range(4):
                value = product[part * rows : (part + 1) * rows]
                prod[piece, 2 * step + part // 2, part % 2] = value
                cast[piece, 2 * step + part // 2, part % 2] = value.astype(jnp.bfloat16)

            @pl.when(step == 0)
            def _():
                for kind in (FAR_UP, FAR_DOWN, OWN_UP):
                    copy_of(kind, piece).start()

            @pl.when(step == 1)
            def _():
                copy_of(OWN_DOWN, piece).start()

    def pass_on(piece):
        for side, (kind, far) in enumerate(((SUM_UP, FAR_UP), (SUM_DOWN, FAR_DOWN))):
            copy_of(far, piece).wait_recv()
            total = prod[piece, 2 * side, side] + gets[piece, far].astype(jnp.float32)
            sums[piece, side] = total.astype(jnp.bfloat16)
            copy_of(kind, piece).start()

    def along_x(piece, y_to):
        return (prod[piece, 3, y_to] + gets[piece, SUM_UP + y_to].astype(jnp.float32)
                + gets[piece, OWN_DOWN - y_to].astype(jnp.float32))

    def cross(piece):
        for kind in (OWN_UP, OWN_DOWN, SUM_UP, SUM_DOWN):
            copy_of(kind, piece).wait_recv()
        sums[piece, 2] = along_x(piece, 1 - y_pos).astype(jnp.bfloat16)
        copy_of(ACROSS, piece).start()
        prod[piece, 3, y_pos] = along_x(piece, y_pos)

    def finish(role):
        scale = counts[role, pl.ds(pl.multiple_of(win * 8, 8), 8), :]
        place = lax.broadcasted_iota(jnp.int32, scale.shape, 1) // chunk_rows
        across_row = pl.ds(pl.multiple_of(role * block_rows, block_rows), block_rows)
        for fine in range(FINE):
            totals = [prod[piece, 3, y_pos, fine * 8 : fine * 8 + 8, across_row]
                      for piece in range(PIECES)]
            for lag in range(COARSE):
                block = None
                for piece, total in enumerate(totals):
                    shift = (piece - lag) * chunk_rows % block_rows
                    moved = pltpu.roll(total, shift, 1) if shift else total
                    block = moved if block is None else jnp.where(place == piece, moved, block)
                start = (lag * FINE + fine) * block_rows
                out_ref[role, :, start : start + block_rows] = (block * scale).astype(
                    jnp.bfloat16)

    waited = 1 if first_hop and not steps[0] else 0

    @pl.loop(0, PIECES)
    def _(piece):
        for role in range(ROUNDS):
            if role >= waited:
                part_copy(role, piece, steps[1]).wait_recv()
            twin_copy(role, piece).start()
        rotate_other(0, piece)

        if first_hop:
            @pl.when(piece < PIECES - 2)
            def _():
                hop_on(piece + 2)

        @pl.when(piece >= 1)
        def _():
            pass_on(piece - 1)

        @pl.when(piece >= 2)
        def _():
            cross(piece - 2)

        for role in range(ROUNDS):
            twin_copy(role, piece).wait_recv()
        rotate_other(1, piece)
        compute(piece)

    pass_on(PIECES - 1)

    @pl.loop(PIECES - 2, PIECES)
    def _(piece):
        cross(piece)

    @pl.loop(0, PIECES)
    def _(piece):
        copy_of(ACROSS, piece).wait_recv()
        prod[piece, 3, y_pos] = prod[piece, 3, y_pos] + gets[piece, ACROSS].astype(jnp.float32)

    @pl.loop(0, ROUNDS)
    def _(role):
        finish(role)

    own_copy.wait_send()

    @pl.loop(0, PIECES)
    def _(index):
        if first_hop:
            hop_copy(index).wait_send()
        for role, flip in enumerate(steps):
            if flip:
                part_copy(role, index, flip).wait_send()
            twin_copy(role, index).wait_send()

    @pl.loop(0, PIECES)
    def _(piece):
        for kind in range(7):
            copy_of(kind, piece).wait_send()


def route_of(flip, blocks):
    flips = (flip, flip ^ (blocks - 1))
    first_hop = flip & ~3 if flip >= 8 else 0
    return flips, first_hop, tuple(each ^ first_hop for each in flips)


def correlate(flip, spectra, masks, cosine, sine):
    block_rows, two_bins = spectra.shape[1:]
    rows = FINE * 8
    bf16, f32 = jnp.bfloat16, jnp.float32
    vmem, dma = pltpu.VMEM, pltpu.SemaphoreType.DMA
    return pl.pallas_call(
        functools.partial(stack_kernel, route_of(flip, lax.axis_size("chan"))),
        name=f"stack_{flip}",
        out_shape=jax.ShapeDtypeStruct((ROUNDS, 8, LAGS * block_rows), bf16),
        in_specs=[pl.BlockSpec(memory_space=vmem)] * 4,
        out_specs=pl.BlockSpec(memory_space=vmem),
        scratch_shapes=[
            vmem((block_rows, 1), f32),
            vmem((ROUNDS, block_rows, block_rows), f32),
            vmem((2, block_rows, two_bins), bf16),
            vmem((2, ROUNDS, block_rows, two_bins), bf16),
            vmem((block_rows, two_bins), bf16),
            vmem((8 * rows, 2 * two_bins), bf16),
            vmem((ROUNDS * COARSE * block_rows, 2 * two_bins), bf16),
            vmem((PIECES, 4, 2, rows, 256), f32),
            vmem((PIECES, 4, 2, rows, 256), bf16),
            vmem((PIECES, 3, rows, 256), bf16),
            vmem((PIECES, 7, rows, 256), bf16),
            dma((2,)),
            dma((PIECES,)),
            dma((PIECES,)),
            dma((ROUNDS, PIECES)),
            dma((ROUNDS, PIECES)),
            dma((ROUNDS, PIECES)),
            dma((ROUNDS, PIECES)),
            dma((PIECES, 7)),
            dma((PIECES, 7)),
        ],
        compiler_params=pltpu.CompilerParams(
            collective_id=flip, has_side_effects=True, vmem_limit_bytes=48 << 20),
    )(spectra, masks, cosine, sine)


def shards(spectra, masks, matching):
    blocks = lax.axis_size("chan")
    cosine, sine = tables(spectra.shape[2] // 2)
    distance = matching[0, 0]
    turned = distance >= blocks // 2
    lower = jnp.where(turned, blocks - 1 - distance, distance)
    branches = [functools.partial(correlate, flip) for flip in range(blocks // 2)]
    result = lax.switch(lower, branches, spectra, masks, jnp.asarray(cosine), jnp.asarray(sine))
    return jnp.where(turned, jnp.flip(result, axis=0), result)


def solution(mesh):
    in_specs = (P("win", "chan", None), P(), P())
    out_specs = P(None, ("chan", "win"), None)
    return jax.shard_map(shards, mesh=mesh, in_specs=in_specs, out_specs=out_specs, check_vma=False)
```
